32 devices in a mesh: span: 4 (over z), wall: 8 (over y, x, core).
Axes of the slice: x: 2, y: 2, z: 4, core: 2. Of those that a mesh axis runs over, the one named last changes fastest.
Arguments:
- random_field: bfloat16 [64, 1536, 4096], P(None, 'wall', 'span'), may hold values from -64 to 64
- half_widths: int32 [2, 1536], replicated, may hold values from 2 to 128, as said below
- time_scale: float32 [1536], P('wall'), may hold values from 4 to 64
- target_rms: float32 [1536], P('wall'), may hold values from 0.2 to 2
- previous_state: float32 [1536, 4096], P('wall', 'span'), may hold values from -4 to 4
Outputs:
- inflow: float32 [64, 1536, 4096], P(None, 'wall', 'span')
- final_state: float32 [1536, 4096], P('wall', 'span')
The draws below stay inside these ranges and needn't reach their ends.
Inputs may be any that keep to these rules, and one draw needn't show every extreme that they name: `half_widths`: row 0 holds each row's wall-normal half-width and row 1 its spanwise one; both rows reach 128.
All inputs are finite; a program needn't handle non-finite values.
Results may differ from the reference program's by a relative error of at most 0.005.
The reference program's roundings to bfloat16 on the way count: a program that leaves them out, or rounds other values in their place, can miss the bound.
Values may be sent and summed in bfloat16 or wider, within the bound.
No kernel may reach another device: no remote copies, remote signals or barrier semaphores. Data moves between devices by JAX's collectives and lax.ppermute only.
A program may use at most 256 MiB of HBM per device.

```python
import math
import jax
import jax.numpy as jnp
from jax import lax

NY = 1536
NZ = 4096
MAXW = 128
PLANES = 64


def draw_random_field(key, part):
    key_values = jax.random.fold_in(key, 11)
    key_columns = jax.random.fold_in(key, 12)
    column_ids = jnp.arange(NZ).astype(jnp.float32)
    column_scale = jnp.sqrt(1.0 + 2.0 * column_ids / NZ) * jax.random.uniform(key_columns, (NZ,), jnp.float32, 0.7, 1.4)
    base = jnp.clip(jax.random.normal(key_values, (PLANES, NY, NZ), jnp.float32), -6.0, 6.0)
    scaled = base * column_scale[None, None, :]
    values = 2.0 * (scaled - jnp.roll(scaled, -1, axis=2))
    return values.astype(jnp.bfloat16)


def draw_half_widths(key, part):
    key_wall = jax.random.fold_in(key, 21)
    key_span = jax.random.fold_in(key, 22)
    key_plant = jax.random.fold_in(key, 23)
    row_ids = jnp.arange(NY, dtype=jnp.int32)
    wall_half = jnp.minimum(MAXW, 2 + 4 * (MAXW - 2) * row_ids // NY + jax.random.randint(key_wall, (NY,), 0, 3, dtype=jnp.int32))
    segment_rows = NY // 16
    planted = jnp.arange(16, dtype=jnp.int32) * segment_rows + jax.random.randint(key_plant, (16,), 0, segment_rows, dtype=jnp.int32)
    chosen = jnp.any(row_ids[:, None] == planted[None, :], axis=1)
    wall_half = jnp.where(chosen, MAXW, wall_half)
    wall_half = jnp.where(row_ids == NY - 1, MAXW, wall_half)
    span_half = jax.random.randint(key_span, (NY,), 2, MAXW + 1, dtype=jnp.int32)
    span_half = jnp.where(row_ids == 0, MAXW, span_half)
    return jnp.stack([wall_half, span_half]).astype(jnp.int32)


def levels(key, dims, cuts, smallest, largest):
    factor_of, own = 1.0, jax.random.fold_in(key, 6)
    for position, blocks in cuts:
        draws = jnp.exp(jax.random.uniform(jax.random.fold_in(own, position), (blocks,), jnp.float32, smallest / len(cuts), largest / len(cuts)))
        factor_of = factor_of * jnp.repeat(draws, dims[position] // blocks).reshape([-1 if axis == position else 1 for axis in range(len(dims))])
    return factor_of


def centred(rng, extent, scale, most, split=(), held_as=jnp.bfloat16):
    array = scale * jax.random.normal(rng, extent, jnp.float32)
    if split:
        array = array * levels(rng, extent, split, -0.22, 0.18)
    return jnp.clip(array, -most, most).astype(held_as)


def setup_inputs(seed: int = 0) -> dict:
    key_list = jax.random.split(jax.random.key(seed), 6)
    random_field = draw_random_field(jax.random.fold_in(key_list[5], 71), 0)
    half_widths = draw_half_widths(jax.random.fold_in(key_list[5], 71), 0)
    time_scale = jnp.clip(jnp.exp(math.log(64.0) - 2.7725887 * jax.random.uniform(key_list[2], (NY,), jnp.float32) ** levels(key_list[2], (NY,), ((0, 8),), -0.2, 0.2)), 4.0, 64.0)
    target_rms = jnp.clip(jnp.exp(math.log(2.0) - 2.3025851 * jax.random.uniform(key_list[3], (NY,), jnp.float32) ** levels(key_list[3], (NY,), ((0, 8),), -0.2, 0.2)), 0.2, 2.0)
    previous_state = centred(key_list[4], (NY, NZ), 0.3, 4.0, ((0, 8), (1, 4)), jnp.float32)
    return {"random_field": random_field, "half_widths": half_widths, "time_scale": time_scale, "target_rms": target_rms, "previous_state": previous_state}


def kernel_norm(half_width):
    spread = jnp.arange(-MAXW, MAXW + 1).astype(jnp.float32)
    widths_f = half_width.astype(jnp.float32)[:, None]
    inside = jnp.abs(spread)[None, :] <= widths_f
    terms = jnp.where(inside, jnp.exp(-math.pi * spread * spread / (widths_f * widths_f)), 0.0)
    return jnp.sqrt(lax.optimization_barrier(jnp.sum(terms, axis=1)))

def kernel_values(half_width, norm_rows, offsets):
    extra = (1,) * (offsets.ndim - 1)
    widths_f = half_width.astype(jnp.float32).reshape(half_width.shape + extra)
    scaled = norm_rows.reshape(norm_rows.shape + extra)
    values = jnp.where(jnp.abs(offsets) <= widths_f, jnp.exp(-0.5 * math.pi * offsets * offsets / (widths_f * widths_f)) / scaled, 0.0)
    return values.astype(jnp.bfloat16)

def wall_matrix(half_all, first_row, row_count):
    offsets = (jnp.arange(row_count + 2 * MAXW)[None, :] - jnp.arange(row_count)[:, None] - MAXW).astype(jnp.float32)
    halves = lax.dynamic_slice_in_dim(half_all, first_row, row_count)
    return kernel_values(halves, kernel_norm(halves), jnp.broadcast_to(offsets, (row_count,) + offsets.shape[1:]))

def reference(random_field, half_widths, time_scale, target_rms, previous_state):
    wall_half = half_widths[0]
    span_half = half_widths[1]
    positions = jnp.arange(NZ)
    circular = jnp.where(positions <= NZ // 2, positions, positions - NZ).astype(jnp.float32)
    span_kernel = kernel_values(span_half, kernel_norm(span_half), jnp.broadcast_to(circular, (NY, NZ))).astype(jnp.float32)
    kernel_freq = jnp.fft.rfft(span_kernel, axis=1)

    def span_filter(one_plane):
        spectrum = jnp.fft.rfft(one_plane.astype(jnp.float32), axis=1)
        return jnp.fft.irfft(spectrum * kernel_freq, n=NZ, axis=1).astype(jnp.bfloat16)
    spanned = lax.map(span_filter, random_field)
    wall_block = math.gcd(NY, 128)
    block_count = NY // wall_block
    matrices = [wall_matrix(wall_half, block_index * wall_block, wall_block).astype(jnp.float32) for block_index in range(block_count)]

    def wall_filter(one_plane):
        padded = jnp.pad(one_plane.astype(jnp.float32), ((MAXW, MAXW), (0, 0)))
        pieces = []
        for block_index in range(block_count):
            window = padded[block_index * wall_block:block_index * wall_block + wall_block + 2 * MAXW]
            pieces.append(jnp.dot(matrices[block_index], window, precision=lax.Precision.HIGHEST, preferred_element_type=jnp.float32))
        return jnp.concatenate(pieces, axis=0).astype(jnp.bfloat16)
    filtered = lax.map(wall_filter, spanned)
    decay_rate = jnp.exp(-math.pi / (2.0 * time_scale))
    noise_gain = jnp.sqrt(1.0 - jnp.exp(-math.pi / time_scale))

    def advance(carried, one_plane):
        carried = decay_rate[:, None] * carried + noise_gain[:, None] * one_plane.astype(jnp.float32)
        energy = lax.optimization_barrier(jnp.mean(carried * carried, axis=1))
        scaled = carried * (target_rms / jnp.sqrt(energy + 1e-06))[:, None]
        return (carried, scaled)
    final_state, inflow = lax.scan(advance, previous_state, filtered)
    return (inflow, final_state)
```

```python
import functools
import math

import jax
import jax.numpy as jnp
from jax import lax
from jax.experimental import pallas as pl
from jax.experimental.pallas import tpu as pltpu
from jax.sharding import PartitionSpec as P

NZ = 4096
MAXW = 128
LANES = 128
ROWS = 16


def extended_2(cells, sides, width):
    for axis, dim in sides:
        count = lax.axis_size(axis)
        head = lax.slice_in_dim(cells, 0, width, axis=dim)
        tail = lax.slice_in_dim(cells, cells.shape[dim] - width, cells.shape[dim], axis=dim)
        cells = jnp.concatenate(
            [
                lax.ppermute(tail, axis, [(i, (i + 1) % count) for i in range(count)]),
                cells,
                lax.ppermute(head, axis, [((i + 1) % count, i) for i in range(count)]),
            ],
            axis=dim,
        )
    return cells


def passed_along(array, axis, by):
    length = lax.axis_size(axis)
    pairs = [(i, i + by) for i in range(length) if 0 <= i + by < length]
    return lax.ppermute(array, axis, pairs)


def kernel_norm(half_width):
    spread = jnp.arange(-MAXW, MAXW + 1).astype(jnp.float32)
    widths_f = half_width.astype(jnp.float32)[:, None]
    inside = jnp.abs(spread)[None, :] <= widths_f
    terms = jnp.where(inside, jnp.exp(-math.pi * spread * spread / (widths_f * widths_f)), 0.0)
    return jnp.sqrt(jnp.sum(terms, axis=1))


def kernel_values(half_width, norm_rows, offsets):
    extra = (1,) * (offsets.ndim - 1)
    widths_f = half_width.astype(jnp.float32).reshape(half_width.shape + extra)
    scaled = norm_rows.reshape(norm_rows.shape + extra)
    values = jnp.where(
        jnp.abs(offsets) <= widths_f,
        jnp.exp(-0.5 * math.pi * offsets * offsets / (widths_f * widths_f)) / scaled,
        0.0,
    )
    return values.astype(jnp.bfloat16)


def wall_matrix(half_all, first_row, row_count):
    offsets = (
        jnp.arange(row_count + 2 * MAXW)[None, :] - jnp.arange(row_count)[:, None] - MAXW
    ).astype(jnp.float32)
    halves = lax.dynamic_slice_in_dim(half_all, first_row, row_count)
    return kernel_values(halves, kernel_norm(halves), offsets)


def combine(earlier, later):
    return (earlier[0] * later[0], later[0] * earlier[1] + later[1])


def plain_body(random_field, half_widths, time_scale, target_rms, previous_state):
    planes, row_count, col_count = random_field.shape
    first_row = lax.axis_index("wall") * row_count
    wall_half = half_widths[0]
    span_local = lax.dynamic_slice_in_dim(half_widths[1], first_row, row_count)
    extended = extended_2(random_field, (("span", 2),), MAXW)
    row_block = math.gcd(row_count, 8)
    block_count = row_count // row_block
    span_cols = col_count + 2 * MAXW
    offsets = (jnp.arange(span_cols)[:, None] - jnp.arange(col_count)[None, :] - MAXW).astype(
        jnp.float32
    )
    norm_local = kernel_norm(span_local)
    by_row = jnp.transpose(extended, (1, 0, 2)).reshape(block_count, row_block, planes, span_cols)

    def span_block(packed):
        noise_rows, half_width, norm_row = packed
        matrix = kernel_values(
            half_width, norm_row, jnp.broadcast_to(offsets, (row_block,) + offsets.shape)
        )
        return jnp.einsum(
            "yjz,ypj->ypz", matrix, noise_rows, preferred_element_type=jnp.float32
        ).astype(jnp.bfloat16)

    spanned = lax.map(
        span_block,
        (
            by_row,
            span_local.reshape(block_count, row_block),
            norm_local.reshape(block_count, row_block),
        ),
    )
    spanned = jnp.transpose(spanned.reshape(row_count, planes, col_count), (1, 0, 2))
    reach_steps = -(-MAXW // row_count)
    lower_rims = []
    upper_rims = []
    for distance in range(1, reach_steps + 1):
        rim_rows = min(row_count, MAXW - (distance - 1) * row_count)
        lower_rims.insert(0, passed_along(spanned[:, row_count - rim_rows :], "wall", distance))
        upper_rims.append(passed_along(spanned[:, :rim_rows], "wall", -distance))
    window = jnp.concatenate(lower_rims + [spanned] + upper_rims, axis=1)
    matrix = wall_matrix(wall_half, first_row, row_count)
    filtered = jnp.einsum("yk,pkz->pyz", matrix, window, preferred_element_type=jnp.float32).astype(
        jnp.bfloat16
    )
    decay_rate = jnp.exp(-math.pi / (2.0 * time_scale))[:, None]
    noise_gain = jnp.sqrt(1.0 - jnp.exp(-math.pi / time_scale))[:, None]
    driven = noise_gain[None] * filtered.astype(jnp.float32)
    driven = jnp.concatenate(
        [driven[:1] + decay_rate[None] * previous_state[None], driven[1:]], axis=0
    )
    factors = jnp.broadcast_to(decay_rate[None], (planes, row_count, 1))
    _, states = lax.associative_scan(combine, (factors, driven), axis=0)
    energy = lax.psum(jnp.sum(states * states, axis=2), "span")
    row_scale = target_rms[None, :] / jnp.sqrt(energy / NZ + 1e-06)
    inflow = states * row_scale[:, :, None]
    return (inflow, states[-1])


def toeplitz(taps):
    rolled = pltpu.roll(
        jnp.broadcast_to(taps, (LANES, 2 * LANES)), 0, 1, stride=1, stride_axis=0
    )
    i = lax.broadcasted_iota(jnp.int32, (LANES, LANES), 0)
    j = lax.broadcasted_iota(jnp.int32, (LANES, LANES), 1)
    outer = rolled[:, LANES:]
    parts = [jnp.where(i >= j, outer, 0.0), rolled[:, :LANES], jnp.where(i <= j, outer, 0.0)]
    return jnp.concatenate([part.astype(jnp.bfloat16) for part in parts], axis=0)


def span_kernel(blocks, direct, flag_ref, taps_ref, left_ref, field_ref, right_ref, *refs):
    head_ref, tail_ref = refs[:2]
    planes, rows, cols = field_ref.shape
    tiles = cols // LANES
    step = pl.program_id(0)
    extended = jnp.concatenate([left_ref[...], field_ref[...], right_ref[...]], axis=2)
    by_row = jnp.swapaxes(extended, 0, 1)
    out = []
    for row in range(rows):
        window = jnp.concatenate(
            [by_row[row, :, t * LANES : (t + 3) * LANES] for t in range(tiles)], axis=0
        )
        wide = jnp.dot(
            window, toeplitz(taps_ref[row : row + 1, :]), preferred_element_type=jnp.float32
        ).astype(jnp.bfloat16)
        out.append(
            jnp.concatenate([wide[t * planes : (t + 1) * planes] for t in range(tiles)], axis=1)
        )
    spanned = jnp.swapaxes(jnp.stack(out, axis=0), 0, 1)
    edge = MAXW // rows
    in_head = step < edge
    in_tail = step >= blocks - edge

    @pl.when(in_head)
    def _():
        head_ref[...] = spanned

    @pl.when(in_tail)
    def _():
        tail_ref[...] = spanned

    if direct < planes:
        use_head = flag_ref[0] == 1

        @pl.when((use_head & in_head) | (jnp.logical_not(use_head) & in_tail))
        def _():
            if direct:
                refs[2][...] = spanned[:direct]
            refs[-1][...] = spanned[direct:]


def span_filter(flag, taps, left, field, right, first, relayed):
    planes = left.shape[0]
    _, row_count, cols = field.shape
    blocks = row_count // ROWS
    edge = MAXW // ROWS

    def head(i, flag_ref):
        return (0, jnp.minimum(i, edge - 1), 0)

    def tail(i, flag_ref):
        return (0, jnp.maximum(i - (blocks - edge), 0), 0)

    def either(i, flag_ref):
        low = jnp.minimum(i, edge - 1)
        high = jnp.maximum(i - (blocks - edge), 0)
        return (0, jnp.where(flag_ref[0] == 1, low, high), 0)

    direct = planes - relayed
    outs = [(planes, head), (planes, tail)]
    if relayed:
        outs += [(direct, either)] if direct else []
        outs += [(relayed, either)]
    side = pl.BlockSpec((planes, ROWS, LANES), lambda i, f: (0, i, 0))
    return pl.pallas_call(
        functools.partial(span_kernel, blocks, direct),
        grid_spec=pltpu.PrefetchScalarGridSpec(
            num_scalar_prefetch=1,
            grid=(blocks,),
            in_specs=[
                pl.BlockSpec((ROWS, 2 * LANES), lambda i, f: (i, 0)),
                side,
                pl.BlockSpec(
                    (pl.Element(planes), pl.Element(ROWS), pl.Element(cols)),
                    lambda i, f: (first, i * ROWS, 0),
                ),
                side,
            ],
            out_specs=[pl.BlockSpec((n, ROWS, cols), m) for n, m in outs],
        ),
        out_shape=[jax.ShapeDtypeStruct((n, MAXW, cols), jnp.bfloat16) for n, m in outs],
        cost_estimate=pl.CostEstimate(
            flops=2 * planes * row_count * cols * 3 * LANES,
            bytes_accessed=5 * planes * row_count * cols,
            transcendentals=0,
        ),
        name="span_filter",
    )(flag, taps, left, field, right)


def wall_kernel(
    group, first, direct, relayed, emit, flag_ref, matrix_ref, decay_ref, gain_ref, start_ref,
    sums_ref, low_ref, head_ref, tail_ref, high_ref, *refs
):
    outs = refs[-4:] if emit else refs[-3:]
    filtered_ref, state_ref, energy_ref = outs[:3]
    row_count, cols = state_ref.shape
    step = pl.program_id(0)
    rest = row_count - MAXW
    wide = 2 * LANES

    @pl.when(step == 0)
    def _():
        state_ref[...] = start_ref[...]
        energy_ref[...] = sums_ref[...]

    decay = decay_ref[...]
    gain = gain_ref[...]
    above = matrix_ref[:, : 2 * MAXW]
    below = matrix_ref[:, 2 * MAXW :]
    lane = lax.broadcasted_iota(jnp.int32, (row_count, LANES), 1)
    for g in range(group):
        total = jnp.zeros((row_count, LANES), jnp.float32)
        for c in range(cols // wide):
            at = slice(c * wide, (c + 1) * wide)
            low = low_ref[g, :, at]
            high = high_ref[g, :, at]
            if relayed:
                crossed = refs[0][g, :, at]
                if direct:
                    crossed = jnp.where(step * group < direct, crossed, refs[1][g, :, at])
                low = jnp.where(flag_ref[0] == 1, crossed, low)
                high = jnp.where(flag_ref[0] == 2, crossed, high)
            upper = jnp.concatenate([low, head_ref[g, :, at]], axis=0)
            lower = jnp.concatenate([tail_ref[g, MAXW - rest :, at], high], axis=0)
            summed = jnp.dot(above, upper, preferred_element_type=jnp.float32) + jnp.dot(
                below, lower, preferred_element_type=jnp.float32
            )
            rounded = summed.astype(jnp.bfloat16)
            filtered_ref[g, :, at] = rounded
            driven = rounded.astype(jnp.float32)
            for h in range(wide // LANES):
                cell = slice(c * wide + h * LANES, c * wide + (h + 1) * LANES)
                state = decay * state_ref[:, cell] + gain * driven[:, h * LANES : (h + 1) * LANES]
                state_ref[:, cell] = state
                total = total + state * state
        sums = jnp.sum(total, axis=1, keepdims=True)
        energy_ref[...] = jnp.where(
            lane == first + step * group + g, sums, energy_ref[...]
        )
    if emit:

        @pl.when(step == pl.num_programs(0) - 1)
        def _():
            outs[3][...] = jnp.transpose(energy_ref[...])[emit[0] : emit[1]]


def wall_filter(flag, matrix, decay, gain, start, sums, first, rims, crossed, emit):
    planes, _, cols = rims[1].shape
    row_count = start.shape[0]
    relayed = crossed[-1].shape[0] if crossed else 0
    direct = planes - relayed
    group = math.gcd(math.gcd(planes, 4), relayed)
    steps = direct // group
    rim = pl.BlockSpec((group, MAXW, cols), lambda p, f: (p, 0, 0))
    whole = lambda a: pl.BlockSpec(a.shape, lambda p, f: (0, 0))
    energy = jax.ShapeDtypeStruct((row_count, LANES), jnp.float32)
    extra = []
    if relayed:
        if direct:
            extra.append(
                pl.BlockSpec(
                    (group, MAXW, cols), lambda p, f: (jnp.minimum(p, steps - 1), 0, 0)
                )
            )
        extra.append(
            pl.BlockSpec((group, MAXW, cols), lambda p, f: (jnp.maximum(p - steps, 0), 0, 0))
        )
    operands = [matrix, decay, gain, start, sums]
    outs = [
        jax.ShapeDtypeStruct((planes, row_count, cols), jnp.bfloat16),
        jax.ShapeDtypeStruct(start.shape, jnp.float32),
        energy,
    ]
    out_specs = [
        pl.BlockSpec((group, row_count, cols), lambda p, f: (p, 0, 0)),
        whole(start),
        whole(energy),
    ]
    if emit:
        outs.append(jax.ShapeDtypeStruct((emit[1] - emit[0], row_count), jnp.float32))
        out_specs.append(whole(outs[-1]))
    return pl.pallas_call(
        functools.partial(wall_kernel, group, first, direct, relayed, emit),
        grid_spec=pltpu.PrefetchScalarGridSpec(
            num_scalar_prefetch=1,
            grid=(planes // group,),
            in_specs=[whole(a) for a in operands] + [rim] * 4 + extra,
            out_specs=out_specs,
        ),
        out_shape=outs,
        cost_estimate=pl.CostEstimate(
            flops=2 * planes * row_count * cols * matrix.shape[1],
            bytes_accessed=8 * planes * row_count * cols,
            transcendentals=0,
        ),
        name="wall_filter",
    )(flag, *operands, *rims, *crossed)


def scale_kernel(
    parts, first, cells, decay_ref, gain_ref, rms_ref, start_ref, filtered_ref, *refs
):
    out_ref, scale_ref = refs[-2:]
    planes, rows, cols = filtered_ref.shape
    step = pl.program_id(0)

    @pl.when(step == 0)
    def _():
        total = refs[0][...]
        for ref in refs[1:parts]:
            total = total + ref[...]
        count, row_count = total.shape
        total = jnp.concatenate(
            [total, jnp.zeros((LANES - count, row_count), jnp.float32)], axis=0
        )
        scale_ref[...] = rms_ref[...] / jnp.sqrt(jnp.transpose(total) / cells + 1e-06)

    scale = scale_ref[pl.ds(step * rows, rows), :]
    wide = [
        jnp.broadcast_to(scale[:, p : p + 1], (rows, LANES))
        for p in range(first, first + planes)
    ]
    decay = decay_ref[...]
    gain = gain_ref[...]
    for c in range(cols // LANES):
        at = slice(c * LANES, (c + 1) * LANES)
        state = start_ref[:, at]
        for p in range(planes):
            state = decay * state + gain * filtered_ref[p, :, at].astype(jnp.float32)
            out_ref[p, :, at] = state * wide[p]


def rescale(decay, gain, rms, start, filtered, energies, offset, target, first, total_planes):
    planes, row_count, cols = filtered.shape
    rows = ROWS * math.gcd(row_count // ROWS, 3)
    narrow = pl.BlockSpec((rows, LANES), lambda i: (i, 0))
    whole = lambda a: pl.BlockSpec(a.shape, lambda i: (0, 0))
    operands = [decay, gain, rms, start, filtered, *energies]
    in_specs = [
        narrow,
        narrow,
        whole(rms),
        pl.BlockSpec((rows, cols), lambda i: (i, 0)),
        pl.BlockSpec((planes, rows, cols), lambda i: (0, i, 0)),
    ] + [whole(e) for e in energies]
    aliases = {}
    if target is not None:
        aliases = {len(operands): 0}
        operands.append(target)
        in_specs.append(pl.BlockSpec(memory_space=pl.ANY))
    return pl.pallas_call(
        functools.partial(scale_kernel, len(energies), first - offset, float(NZ)),
        grid=(row_count // rows,),
        in_specs=in_specs,
        out_specs=pl.BlockSpec(
            (pl.Element(planes), pl.Element(rows), pl.Element(cols)),
            lambda i: (first, i * rows, 0),
        ),
        out_shape=jax.ShapeDtypeStruct((total_planes, row_count, cols), jnp.float32),
        scratch_shapes=[pltpu.VMEM((row_count, LANES), jnp.float32)],
        input_output_aliases=aliases,
        cost_estimate=pl.CostEstimate(
            flops=4 * planes * row_count * cols,
            bytes_accessed=6 * planes * row_count * cols,
            transcendentals=0,
        ),
        name="rescale",
    )(*operands)


def span_taps(half_width):
    place = jnp.arange(2 * LANES)
    offsets = jnp.where(place <= LANES, place, place - 2 * LANES).astype(jnp.float32)
    values = kernel_values(half_width, kernel_norm(half_width), offsets[None, :])
    return values.astype(jnp.float32)


def neighbour_pairs(count, by, skip=()):
    return [
        (i, i + by) for i in range(count) if 0 <= i + by < count and (i, i + by) not in skip
    ]


CHUNKS = (8, 12, 16, 16, 12)
RELAYED = (0, 12, 12, 8, 0)
SUMMED = (1, 2, 3, 4)
ORDER = (
    "H0 H1 S0 U0",
    "D0 H2 S1 H3",
    "V1 U1 D1 S2",
    "V2 U2 D2 Q2",
    "X1 H4 S3 V3",
    "U3 D3 Q3 W0",
    "S4 X2 U4 D4",
    "X3 W1 E1 F0",
    "F1 W2 E2 F2",
    "W3 E3 F3 W4",
    "E4 F4",
)


def relay_plan(walls):
    return RELAYED if walls == 8 else (0,) * len(CHUNKS)


def sequence(relayed, spans):
    names = []
    for item in " ".join(ORDER).split():
        kind, c = item[0], int(item[1:])
        if kind == "H":
            names += [item + "l", item + "r"]
        elif kind == "E":
            names += [f"{item}s{s}" for s in range(1, spans)]
        elif kind in "VX":
            names += [item] if relayed[c] else []
        elif kind == "Q":
            names += [item] if 0 < relayed[c] < CHUNKS[c] else []
        else:
            names.append(item)
    return names


def body(random_field, half_widths, time_scale, target_rms, previous_state):
    planes, row_count, cols = random_field.shape
    spans = lax.axis_size("span")
    walls = lax.axis_size("wall")
    here = lax.axis_index("wall")
    first_row = here * row_count
    middle = walls // 2
    relayed = relay_plan(walls)
    firsts = [sum(CHUNKS[:c]) for c in range(len(CHUNKS))]

    span_local = lax.dynamic_slice_in_dim(half_widths[1], first_row, row_count)
    taps = span_taps(span_local)
    matrix = wall_matrix(half_widths[0], first_row, row_count)
    spread = lambda v: jnp.broadcast_to(v[:, None], (row_count, LANES))
    decay = spread(jnp.exp(-math.pi / (2.0 * time_scale)))
    gain = spread(jnp.sqrt(1.0 - jnp.exp(-math.pi / time_scale)))
    rms = spread(target_rms)
    flag = jnp.where(here == middle, 1, jnp.where(here == middle - 1, 2, 0)).astype(jnp.int32)
    flag = flag.reshape(1)

    crossing = ((middle - 1, middle), (middle, middle - 1))
    made = {}
    states = [previous_state]
    sums = jnp.zeros((row_count, LANES), jnp.float32)
    target = None
    for name in sequence(relayed, spans):
        kind, c = name[0], int(name[1:2])
        first, size = firsts[c], CHUNKS[c]
        skip = crossing if relayed[c] else ()
        if kind == "H":
            part = lax.slice_in_dim(random_field, first, first + size, axis=0)
            if name.endswith("l"):
                edge = part[:, :, cols - MAXW :]
                pairs = [(i, (i + 1) % spans) for i in range(spans)]
            else:
                edge = part[:, :, :MAXW]
                pairs = [((i + 1) % spans, i) for i in range(spans)]
            made[name] = lax.ppermute(edge, "span", pairs)
        elif kind == "S":
            left, right = made[f"H{c}l"], made[f"H{c}r"]
            made[name] = span_filter(
                flag, taps, left, random_field, right, first, relayed[c]
            )
        elif kind == "U":
            tail = made[f"S{c}"][1]
            made[name] = lax.ppermute(tail, "wall", neighbour_pairs(walls, 1, skip))
        elif kind == "D":
            head = made[f"S{c}"][0]
            made[name] = lax.ppermute(head, "wall", neighbour_pairs(walls, -1, skip))
        elif kind == "Q":
            made[name] = lax.ppermute(made[f"S{c}"][2], "wall", crossing)
        elif kind == "V":
            out = [(middle - 1, walls - 1), (middle, 0)]
            made[name] = lax.ppermute(made[f"S{c}"][-1], "wall", out)
        elif kind == "X":
            back = [(walls - 1, middle), (0, middle - 1)]
            made[name] = lax.ppermute(made[f"V{c}"], "wall", back)
        elif kind == "W":
            head, tail = made[f"S{c}"][:2]
            rims = (made[f"U{c}"], head, tail, made[f"D{c}"])
            crossed = [made[k] for k in (f"Q{c}", f"X{c}") if k in made]
            emit = None
            if c in SUMMED:
                start = max([firsts[e + 1] for e in SUMMED if e < c], default=0)
                emit = (start // 8 * 8, -(-(first + size) // 8) * 8)
            made[name], state, sums, *out = wall_filter(
                flag, matrix, decay, gain, states[c], sums, first, rims, crossed, emit
            )
            states.append(state)
            if emit:
                made[f"E{c}"] = (emit[0], out)
        elif kind == "E":
            by = int(name.split("s")[1])
            pairs = [(i, (i + by) % spans) for i in range(spans)]
            energies = made[f"E{c}"][1]
            energies.append(lax.ppermute(energies[0], "span", pairs))
        else:
            offset, energies = made[f"E{min(e for e in SUMMED if e >= c)}"]
            filtered = made[f"W{c}"]
            target = rescale(
                decay, gain, rms, states[c], filtered, energies, offset, target, first, planes
            )
    return (target, states[-1])


def solution(mesh):
    in_specs = (P(None, "wall", "span"), P(), P("wall"), P("wall"), P("wall", "span"))
    out_specs = (P(None, "wall", "span"), P("wall", "span"))

    def step(random_field, *rest):
        planes, row_count, cols = random_field.shape
        fits = MAXW <= row_count <= 2 * MAXW and row_count % ROWS == 0
        fits = fits and planes == sum(CHUNKS) and cols % (2 * LANES) == 0
        return (body if fits else plain_body)(random_field, *rest)

    return jax.shard_map(
        step, mesh=mesh, in_specs=in_specs, out_specs=out_specs, check_vma=False
    )
```

```python
import functools
import math

import jax
import jax.numpy as jnp
from jax import lax
from jax.experimental import pallas as pl
from jax.experimental.pallas import tpu as pltpu
from jax.sharding import PartitionSpec as P

NZ = 4096
MAXW = 128
LANES = 128
ROWS = 16


def extended_2(cells, sides, width):
    for axis, dim in sides:
        count = lax.axis_size(axis)
        head = lax.slice_in_dim(cells, 0, width, axis=dim)
        tail = lax.slice_in_dim(cells, cells.shape[dim] - width, cells.shape[dim], axis=dim)
        cells = jnp.concatenate(
            [
                lax.ppermute(tail, axis, [(i, (i + 1) % count) for i in range(count)]),
                cells,
                lax.ppermute(head, axis, [((i + 1) % count, i) for i in range(count)]),
            ],
            axis=dim,
        )
    return cells


def passed_along(array, axis, by):
    length = lax.axis_size(axis)
    pairs = [(i, i + by) for i in range(length) if 0 <= i + by < length]
    return lax.ppermute(array, axis, pairs)


def kernel_norm(half_width):
    spread = jnp.arange(-MAXW, MAXW + 1).astype(jnp.float32)
    widths_f = half_width.astype(jnp.float32)[:, None]
    inside = jnp.abs(spread)[None, :] <= widths_f
    terms = jnp.where(inside, jnp.exp(-math.pi * spread * spread / (widths_f * widths_f)), 0.0)
    return jnp.sqrt(jnp.sum(terms, axis=1))


def kernel_values(half_width, norm_rows, offsets):
    extra = (1,) * (offsets.ndim - 1)
    widths_f = half_width.astype(jnp.float32).reshape(half_width.shape + extra)
    scaled = norm_rows.reshape(norm_rows.shape + extra)
    values = jnp.where(
        jnp.abs(offsets) <= widths_f,
        jnp.exp(-0.5 * math.pi * offsets * offsets / (widths_f * widths_f)) / scaled,
        0.0,
    )
    return values.astype(jnp.bfloat16)


def wall_matrix(half_all, first_row, row_count):
    offsets = (
        jnp.arange(row_count + 2 * MAXW)[None, :] - jnp.arange(row_count)[:, None] - MAXW
    ).astype(jnp.float32)
    halves = lax.dynamic_slice_in_dim(half_all, first_row, row_count)
    return kernel_values(halves, kernel_norm(halves), offsets)


def combine(earlier, later):
    return (earlier[0] * later[0], later[0] * earlier[1] + later[1])


def plain_body(random_field, half_widths, time_scale, target_rms, previous_state):
    planes, row_count, col_count = random_field.shape
    first_row = lax.axis_index("wall") * row_count
    wall_half = half_widths[0]
    span_local = lax.dynamic_slice_in_dim(half_widths[1], first_row, row_count)
    extended = extended_2(random_field, (("span", 2),), MAXW)
    row_block = math.gcd(row_count, 8)
    block_count = row_count // row_block
    span_cols = col_count + 2 * MAXW
    offsets = (jnp.arange(span_cols)[:, None] - jnp.arange(col_count)[None, :] - MAXW).astype(
        jnp.float32
    )
    norm_local = kernel_norm(span_local)
    by_row = jnp.transpose(extended, (1, 0, 2)).reshape(block_count, row_block, planes, span_cols)

    def span_block(packed):
        noise_rows, half_width, norm_row = packed
        matrix = kernel_values(
            half_width, norm_row, jnp.broadcast_to(offsets, (row_block,) + offsets.shape)
        )
        return jnp.einsum(
            "yjz,ypj->ypz", matrix, noise_rows, preferred_element_type=jnp.float32
        ).astype(jnp.bfloat16)

    spanned = lax.map(
        span_block,
        (
            by_row,
            span_local.reshape(block_count, row_block),
            norm_local.reshape(block_count, row_block),
        ),
    )
    spanned = jnp.transpose(spanned.reshape(row_count, planes, col_count), (1, 0, 2))
    reach_steps = -(-MAXW // row_count)
    lower_rims = []
    upper_rims = []
    for distance in range(1, reach_steps + 1):
        rim_rows = min(row_count, MAXW - (distance - 1) * row_count)
        lower_rims.insert(0, passed_along(spanned[:, row_count - rim_rows :], "wall", distance))
        upper_rims.append(passed_along(spanned[:, :rim_rows], "wall", -distance))
    window = jnp.concatenate(lower_rims + [spanned] + upper_rims, axis=1)
    matrix = wall_matrix(wall_half, first_row, row_count)
    filtered = jnp.einsum("yk,pkz->pyz", matrix, window, preferred_element_type=jnp.float32).astype(
        jnp.bfloat16
    )
    decay_rate = jnp.exp(-math.pi / (2.0 * time_scale))[:, None]
    noise_gain = jnp.sqrt(1.0 - jnp.exp(-math.pi / time_scale))[:, None]
    driven = noise_gain[None] * filtered.astype(jnp.float32)
    driven = jnp.concatenate(
        [driven[:1] + decay_rate[None] * previous_state[None], driven[1:]], axis=0
    )
    factors = jnp.broadcast_to(decay_rate[None], (planes, row_count, 1))
    _, states = lax.associative_scan(combine, (factors, driven), axis=0)
    energy = lax.psum(jnp.sum(states * states, axis=2), "span")
    row_scale = target_rms[None, :] / jnp.sqrt(energy / NZ + 1e-06)
    inflow = states * row_scale[:, :, None]
    return (inflow, states[-1])


def toeplitz(taps):
    rolled = pltpu.roll(
        jnp.broadcast_to(taps, (LANES, 2 * LANES)), 0, 1, stride=1, stride_axis=0
    )
    i = lax.broadcasted_iota(jnp.int32, (LANES, LANES), 0)
    j = lax.broadcasted_iota(jnp.int32, (LANES, LANES), 1)
    outer = rolled[:, LANES:]
    parts = [jnp.where(i >= j, outer, 0.0), rolled[:, :LANES], jnp.where(i <= j, outer, 0.0)]
    return jnp.concatenate([part.astype(jnp.bfloat16) for part in parts], axis=0)


def span_kernel(blocks, direct, flag_ref, taps_ref, left_ref, field_ref, right_ref, *refs):
    head_ref, tail_ref = refs[:2]
    planes, rows, cols = field_ref.shape
    tiles = cols // LANES
    step = pl.program_id(0)
    extended = jnp.concatenate([left_ref[...], field_ref[...], right_ref[...]], axis=2)
    by_row = jnp.swapaxes(extended, 0, 1)
    out = []
    for row in range(rows):
        window = jnp.concatenate(
            [by_row[row, :, t * LANES : (t + 3) * LANES] for t in range(tiles)], axis=0
        )
        wide = jnp.dot(
            window, toeplitz(taps_ref[row : row + 1, :]), preferred_element_type=jnp.float32
        ).astype(jnp.bfloat16)
        out.append(
            jnp.concatenate([wide[t * planes : (t + 1) * planes] for t in range(tiles)], axis=1)
        )
    spanned = jnp.swapaxes(jnp.stack(out, axis=0), 0, 1)
    edge = MAXW // rows
    in_head = step < edge
    in_tail = step >= blocks - edge

    @pl.when(in_head)
    def _():
        head_ref[...] = spanned

    @pl.when(in_tail)
    def _():
        tail_ref[...] = spanned

    if direct < planes:
        use_head = flag_ref[0] == 1

        @pl.when((use_head & in_head) | (jnp.logical_not(use_head) & in_tail))
        def _():
            if direct:
                refs[2][...] = spanned[:direct]
            refs[-1][...] = spanned[direct:]


def span_filter(flag, taps, left, field, right, first, relayed):
    planes = left.shape[0]
    _, row_count, cols = field.shape
    blocks = row_count // ROWS
    edge = MAXW // ROWS

    def head(i, flag_ref):
        return (0, jnp.minimum(i, edge - 1), 0)

    def tail(i, flag_ref):
        return (0, jnp.maximum(i - (blocks - edge), 0), 0)

    def either(i, flag_ref):
        low = jnp.minimum(i, edge - 1)
        high = jnp.maximum(i - (blocks - edge), 0)
        return (0, jnp.where(flag_ref[0] == 1, low, high), 0)

    direct = planes - relayed
    outs = [(planes, head), (planes, tail)]
    if relayed:
        outs += [(direct, either)] if direct else []
        outs += [(relayed, either)]
    side = pl.BlockSpec((planes, ROWS, LANES), lambda i, f: (0, i, 0))
    return pl.pallas_call(
        functools.partial(span_kernel, blocks, direct),
        grid_spec=pltpu.PrefetchScalarGridSpec(
            num_scalar_prefetch=1,
            grid=(blocks,),
            in_specs=[
                pl.BlockSpec((ROWS, 2 * LANES), lambda i, f: (i, 0)),
                side,
                pl.BlockSpec(
                    (pl.Element(planes), pl.Element(ROWS), pl.Element(cols)),
                    lambda i, f: (first, i * ROWS, 0),
                ),
                side,
            ],
            out_specs=[pl.BlockSpec((n, ROWS, cols), m) for n, m in outs],
        ),
        out_shape=[jax.ShapeDtypeStruct((n, MAXW, cols), jnp.bfloat16) for n, m in outs],
        cost_estimate=pl.CostEstimate(
            flops=2 * planes * row_count * cols * 3 * LANES,
            bytes_accessed=5 * planes * row_count * cols,
            transcendentals=0,
        ),
        name="span_filter",
    )(flag, taps, left, field, right)


def wall_kernel(
    group, first, direct, relayed, emit, flag_ref, matrix_ref, decay_ref, gain_ref, start_ref,
    sums_ref, low_ref, head_ref, tail_ref, high_ref, *refs
):
    outs = refs[-4:] if emit else refs[-3:]
    filtered_ref, state_ref, energy_ref = outs[:3]
    row_count, cols = state_ref.shape
    step = pl.program_id(0)
    rest = row_count - MAXW
    wide = 2 * LANES

    @pl.when(step == 0)
    def _():
        state_ref[...] = start_ref[...]
        energy_ref[...] = sums_ref[...]

    decay = decay_ref[...]
    gain = gain_ref[...]
    above = matrix_ref[:, : 2 * MAXW]
    below = matrix_ref[:, 2 * MAXW :]
    lane = lax.broadcasted_iota(jnp.int32, (row_count, LANES), 1)
    for g in range(group):
        total = jnp.zeros((row_count, LANES), jnp.float32)
        for c in range(cols // wide):
            at = slice(c * wide, (c + 1) * wide)
            low = low_ref[g, :, at]
            high = high_ref[g, :, at]
            if relayed:
                crossed = refs[0][g, :, at]
                if direct:
                    crossed = jnp.where(step * group < direct, crossed, refs[1][g, :, at])
                low = jnp.where(flag_ref[0] == 1, crossed, low)
                high = jnp.where(flag_ref[0] == 2, crossed, high)
            upper = jnp.concatenate([low, head_ref[g, :, at]], axis=0)
            lower = jnp.concatenate([tail_ref[g, MAXW - rest :, at], high], axis=0)
            summed = jnp.dot(above, upper, preferred_element_type=jnp.float32) + jnp.dot(
                below, lower, preferred_element_type=jnp.float32
            )
            rounded = summed.astype(jnp.bfloat16)
            filtered_ref[g, :, at] = rounded
            driven = rounded.astype(jnp.float32)
            for h in range(wide // LANES):
                cell = slice(c * wide + h * LANES, c * wide + (h + 1) * LANES)
                state = decay * state_ref[:, cell] + gain * driven[:, h * LANES : (h + 1) * LANES]
                state_ref[:, cell] = state
                total = total + state * state
        sums = jnp.sum(total, axis=1, keepdims=True)
        energy_ref[...] = jnp.where(
            lane == first + step * group + g, sums, energy_ref[...]
        )
    if emit:

        @pl.when(step == pl.num_programs(0) - 1)
        def _():
            outs[3][...] = jnp.transpose(energy_ref[...])[emit[0] : emit[1]]


def wall_filter(flag, matrix, decay, gain, start, sums, first, rims, crossed, emit):
    planes, _, cols = rims[1].shape
    row_count = start.shape[0]
    relayed = crossed[-1].shape[0] if crossed else 0
    direct = planes - relayed
    group = math.gcd(math.gcd(planes, 4), relayed)
    steps = direct // group
    rim = pl.BlockSpec((group, MAXW, cols), lambda p, f: (p, 0, 0))
    whole = lambda a: pl.BlockSpec(a.shape, lambda p, f: (0, 0))
    energy = jax.ShapeDtypeStruct((row_count, LANES), jnp.float32)
    extra = []
    if relayed:
        if direct:
            extra.append(
                pl.BlockSpec(
                    (group, MAXW, cols), lambda p, f: (jnp.minimum(p, steps - 1), 0, 0)
                )
            )
        extra.append(
            pl.BlockSpec((group, MAXW, cols), lambda p, f: (jnp.maximum(p - steps, 0), 0, 0))
        )
    operands = [matrix, decay, gain, start, sums]
    outs = [
        jax.ShapeDtypeStruct((planes, row_count, cols), jnp.bfloat16),
        jax.ShapeDtypeStruct(start.shape, jnp.float32),
        energy,
    ]
    out_specs = [
        pl.BlockSpec((group, row_count, cols), lambda p, f: (p, 0, 0)),
        whole(start),
        whole(energy),
    ]
    if emit:
        outs.append(jax.ShapeDtypeStruct((emit[1] - emit[0], row_count), jnp.float32))
        out_specs.append(whole(outs[-1]))
    return pl.pallas_call(
        functools.partial(wall_kernel, group, first, direct, relayed, emit),
        grid_spec=pltpu.PrefetchScalarGridSpec(
            num_scalar_prefetch=1,
            grid=(planes // group,),
            in_specs=[whole(a) for a in operands] + [rim] * 4 + extra,
            out_specs=out_specs,
        ),
        out_shape=outs,
        cost_estimate=pl.CostEstimate(
            flops=2 * planes * row_count * cols * matrix.shape[1],
            bytes_accessed=8 * planes * row_count * cols,
            transcendentals=0,
        ),
        name="wall_filter",
    )(flag, *operands, *rims, *crossed)


def scale_kernel(
    parts, first, cells, decay_ref, gain_ref, rms_ref, start_ref, filtered_ref, *refs
):
    out_ref, scale_ref = refs[-2:]
    planes, rows, cols = filtered_ref.shape
    step = pl.program_id(0)

    @pl.when(step == 0)
    def _():
        total = refs[0][...]
        for ref in refs[1:parts]:
            total = total + ref[...]
        count, row_count = total.shape
        total = jnp.concatenate(
            [total, jnp.zeros((LANES - count, row_count), jnp.float32)], axis=0
        )
        scale_ref[...] = rms_ref[...] / jnp.sqrt(jnp.transpose(total) / cells + 1e-06)

    scale = scale_ref[pl.ds(step * rows, rows), :]
    wide = [
        jnp.broadcast_to(scale[:, p : p + 1], (rows, LANES))
        for p in range(first, first + planes)
    ]
    decay = decay_ref[...]
    gain = gain_ref[...]
    for c in range(cols // LANES):
        at = slice(c * LANES, (c + 1) * LANES)
        state = start_ref[:, at]
        for p in range(planes):
            state = decay * state + gain * filtered_ref[p, :, at].astype(jnp.float32)
            out_ref[p, :, at] = state * wide[p]


def rescale(decay, gain, rms, start, filtered, energies, offset, target, first, total_planes):
    planes, row_count, cols = filtered.shape
    rows = ROWS * math.gcd(row_count // ROWS, 3)
    narrow = pl.BlockSpec((rows, LANES), lambda i: (i, 0))
    whole = lambda a: pl.BlockSpec(a.shape, lambda i: (0, 0))
    operands = [decay, gain, rms, start, filtered, *energies]
    in_specs = [
        narrow,
        narrow,
        whole(rms),
        pl.BlockSpec((rows, cols), lambda i: (i, 0)),
        pl.BlockSpec((planes, rows, cols), lambda i: (0, i, 0)),
    ] + [whole(e) for e in energies]
    aliases = {}
    if target is not None:
        aliases = {len(operands): 0}
        operands.append(target)
        in_specs.append(pl.BlockSpec(memory_space=pl.ANY))
    return pl.pallas_call(
        functools.partial(scale_kernel, len(energies), first - offset, float(NZ)),
        grid=(row_count // rows,),
        in_specs=in_specs,
        out_specs=pl.BlockSpec(
            (pl.Element(planes), pl.Element(rows), pl.Element(cols)),
            lambda i: (first, i * rows, 0),
        ),
        out_shape=jax.ShapeDtypeStruct((total_planes, row_count, cols), jnp.float32),
        scratch_shapes=[pltpu.VMEM((row_count, LANES), jnp.float32)],
        input_output_aliases=aliases,
        cost_estimate=pl.CostEstimate(
            flops=4 * planes * row_count * cols,
            bytes_accessed=6 * planes * row_count * cols,
            transcendentals=0,
        ),
        name="rescale",
    )(*operands)


def span_taps(half_width):
    place = jnp.arange(2 * LANES)
    offsets = jnp.where(place <= LANES, place, place - 2 * LANES).astype(jnp.float32)
    values = kernel_values(half_width, kernel_norm(half_width), offsets[None, :])
    return values.astype(jnp.float32)


def neighbour_pairs(count, by, skip=()):
    return [
        (i, i + by) for i in range(count) if 0 <= i + by < count and (i, i + by) not in skip
    ]


CHUNKS = (8, 12, 16, 16, 12)
RELAYED = (0, 12, 12, 6, 0)
SUMMED = (1, 2, 3, 4)
ORDER = (
    "H0 H1 S0 U0",
    "D0 H2 S1 U1",
    "D1 V1 H3 S2",
    "V2 U2 D2 Q2",
    "X1 H4 S3 V3",
    "U3 D3 Q3 W0",
    "S4 X2 U4 D4",
    "X3 W1 E1 F0",
    "F1 W2 E2 F2",
    "W3 E3 F3 W4",
    "E4 F4",
)


def relay_plan(walls):
    return RELAYED if walls == 8 else (0,) * len(CHUNKS)


def sequence(relayed, spans):
    names = []
    for item in " ".join(ORDER).split():
        kind, c = item[0], int(item[1:])
        if kind == "H":
            names += [item + "l", item + "r"]
        elif kind == "E":
            names += [f"{item}s{s}" for s in range(1, spans)]
        elif kind in "VX":
            names += [item] if relayed[c] else []
        elif kind == "Q":
            names += [item] if 0 < relayed[c] < CHUNKS[c] else []
        else:
            names.append(item)
    return names


def body(random_field, half_widths, time_scale, target_rms, previous_state):
    planes, row_count, cols = random_field.shape
    spans = lax.axis_size("span")
    walls = lax.axis_size("wall")
    here = lax.axis_index("wall")
    first_row = here * row_count
    middle = walls // 2
    relayed = relay_plan(walls)
    firsts = [sum(CHUNKS[:c]) for c in range(len(CHUNKS))]

    span_local = lax.dynamic_slice_in_dim(half_widths[1], first_row, row_count)
    taps = span_taps(span_local)
    matrix = wall_matrix(half_widths[0], first_row, row_count)
    spread = lambda v: jnp.broadcast_to(v[:, None], (row_count, LANES))
    decay = spread(jnp.exp(-math.pi / (2.0 * time_scale)))
    gain = spread(jnp.sqrt(1.0 - jnp.exp(-math.pi / time_scale)))
    rms = spread(target_rms)
    flag = jnp.where(here == middle, 1, jnp.where(here == middle - 1, 2, 0)).astype(jnp.int32)
    flag = flag.reshape(1)

    crossing = ((middle - 1, middle), (middle, middle - 1))
    made = {}
    states = [previous_state]
    sums = jnp.zeros((row_count, LANES), jnp.float32)
    target = None
    for name in sequence(relayed, spans):
        kind, c = name[0], int(name[1:2])
        first, size = firsts[c], CHUNKS[c]
        skip = crossing if relayed[c] else ()
        if kind == "H":
            part = lax.slice_in_dim(random_field, first, first + size, axis=0)
            if name.endswith("l"):
                edge = part[:, :, cols - MAXW :]
                pairs = [(i, (i + 1) % spans) for i in range(spans)]
            else:
                edge = part[:, :, :MAXW]
                pairs = [((i + 1) % spans, i) for i in range(spans)]
            made[name] = lax.ppermute(edge, "span", pairs)
        elif kind == "S":
            left, right = made[f"H{c}l"], made[f"H{c}r"]
            made[name] = span_filter(
                flag, taps, left, random_field, right, first, relayed[c]
            )
        elif kind == "U":
            tail = made[f"S{c}"][1]
            made[name] = lax.ppermute(tail, "wall", neighbour_pairs(walls, 1, skip))
        elif kind == "D":
            head = made[f"S{c}"][0]
            made[name] = lax.ppermute(head, "wall", neighbour_pairs(walls, -1, skip))
        elif kind == "Q":
            made[name] = lax.ppermute(made[f"S{c}"][2], "wall", crossing)
        elif kind == "V":
            out = [(middle - 1, walls - 1), (middle, 0)]
            made[name] = lax.ppermute(made[f"S{c}"][-1], "wall", out)
        elif kind == "X":
            back = [(walls - 1, middle), (0, middle - 1)]
            made[name] = lax.ppermute(made[f"V{c}"], "wall", back)
        elif kind == "W":
            head, tail = made[f"S{c}"][:2]
            rims = (made[f"U{c}"], head, tail, made[f"D{c}"])
            crossed = [made[k] for k in (f"Q{c}", f"X{c}") if k in made]
            emit = None
            if c in SUMMED:
                start = max([firsts[e + 1] for e in SUMMED if e < c], default=0)
                emit = (start // 8 * 8, -(-(first + size) // 8) * 8)
            made[name], state, sums, *out = wall_filter(
                flag, matrix, decay, gain, states[c], sums, first, rims, crossed, emit
            )
            states.append(state)
            if emit:
                made[f"E{c}"] = (emit[0], out)
        elif kind == "E":
            by = int(name.split("s")[1])
            pairs = [(i, (i + by) % spans) for i in range(spans)]
            energies = made[f"E{c}"][1]
            energies.append(lax.ppermute(energies[0], "span", pairs))
        else:
            offset, energies = made[f"E{min(e for e in SUMMED if e >= c)}"]
            filtered = made[f"W{c}"]
            target = rescale(
                decay, gain, rms, states[c], filtered, energies, offset, target, first, planes
            )
    return (target, states[-1])


def solution(mesh):
    in_specs = (P(None, "wall", "span"), P(), P("wall"), P("wall"), P("wall", "span"))
    out_specs = (P(None, "wall", "span"), P("wall", "span"))

    def step(random_field, *rest):
        planes, row_count, cols = random_field.shape
        fits = MAXW <= row_count <= 2 * MAXW and row_count % ROWS == 0
        fits = fits and planes == sum(CHUNKS) and cols % (2 * LANES) == 0
        return (body if fits else plain_body)(random_field, *rest)

    return jax.shard_map(
        step, mesh=mesh, in_specs=in_specs, out_specs=out_specs, check_vma=False
    )
```
